32 devices in a mesh: mesh: 8 (over z, y), mode: 4 (over x, core).
Axes of the slice: x: 2, y: 2, z: 4, core: 2. Of those that a mesh axis runs over, the one named last changes fastest.
Arguments:
- field: float32 [256, 131072], P('mode', 'mesh'), may hold values from -6 to 6
- right_side: float32 [256, 131072], P('mode', 'mesh'), may hold values from -6 to 6
- coefficient: float32 [2, 131072], P(None, 'mesh'), may hold values from 0.3 to 3
- precond: float32 [131072], P('mesh'), may hold values from 0.1 to 1
- blocks: bfloat16 [2, 7, 256, 256], replicated, may hold values from -0.125 to 0.125
- couplings: int32 [512, 7], P('mesh'), may hold values from 0 to 1, as said below
- chaos_values: bfloat16 [48, 16, 16], replicated, may hold values from -0.875 to 0.875
- chaos_index: int32 [48, 2], replicated, may hold values from 0 to 15, as said below
Outputs:
- updated: float32 [256, 131072], P('mode', 'mesh')
- residual: float32 [256, 131072], P('mode', 'mesh')
The draws below stay inside these ranges and needn't reach their ends.
Inputs may be any that keep to these rules, and one draw needn't show every extreme that they name: couplings[i, c] links block i to block i + c - 3; it is 1 for c = 3 and wherever block i + c - 3 lies in another slab of 16384 unknowns. `chaos_index`: rows 3 r to 3 r + 2 hold row block r, with column blocks r and two other distinct blocks.
All inputs are finite; a program needn't handle non-finite values.
Results may differ from the reference program's by a relative error of at most 0.0032.
Values may be sent and summed in bfloat16 or wider, within the bound.
A program may use at most 128 MiB of HBM per device.

```python
import math
import jax
import jax.numpy as jnp

P_SIZE = 256
PBLK = 16
B = 256
S_DEV = 16384
PB = 16
NNZB = 48
N = 131072
NBLK = 512


def draw_couplings(key, part):
    coin_flip = jax.random.randint(key, (NBLK, 7), 0, 4)
    kept_links = (coin_flip > 0).astype(jnp.int32)
    in_slab = jnp.arange(NBLK, dtype=jnp.int32) % (S_DEV // B)
    offsets = jnp.arange(7, dtype=jnp.int32)
    target = in_slab[:, None] + offsets[None, :] - 3
    forced = (target < 0) | (target >= S_DEV // B) | (offsets[None, :] == 3)
    return jnp.where(forced, 1, kept_links).astype(jnp.int32)


def pick_shifts(row_key):
    return jax.random.permutation(row_key, PBLK - 1)[:2].astype(jnp.int32) + 1


def draw_chaos_index(key, part):
    row_keys = jax.random.split(jax.random.fold_in(key, 7), PBLK)
    shifts = jax.vmap(pick_shifts)(row_keys)
    row_ids = jnp.arange(PBLK, dtype=jnp.int32)
    columns = jnp.stack([row_ids, (row_ids + shifts[:, 0]) % PBLK, (row_ids + shifts[:, 1]) % PBLK], axis=1)
    repeated = jnp.broadcast_to(row_ids[:, None], (PBLK, 3))
    return jnp.stack([repeated, columns], axis=2).reshape(NNZB, 2).astype(jnp.int32)


def level_of(rng, dims, shards, smallest, high):
    def one(axis_at, blocks):
        heights = jax.random.uniform(jax.random.fold_in(jax.random.fold_in(rng, 6), axis_at), (blocks,), jnp.float32, smallest / len(shards), high / len(shards))
        return jnp.repeat(jnp.exp(heights), dims[axis_at] // blocks).reshape((-1,) + (1,) * (len(dims) - axis_at - 1))

    factor_of = one(*shards[0])
    for cut in shards[1:]:
        factor_of = factor_of * one(*cut)
    return factor_of


def noise(stream_key, shape, scale, limit, pieces=(), held_as=jnp.bfloat16):
    entries = scale * jax.random.normal(stream_key, shape, jnp.float32)
    if pieces:
        entries = entries * level_of(stream_key, shape, pieces, -0.22, 0.18)
    return jnp.clip(entries, -limit, limit).astype(held_as)


def setup_inputs(seed: int = 0) -> dict:
    key_list = jax.random.split(jax.random.key(seed), 9)
    field = noise(key_list[0], (P_SIZE, N), 1.0, 6.0, ((0, 4), (1, 8)), jnp.float32)
    right_side = noise(key_list[1], (P_SIZE, N), 1.0, 6.0, ((0, 4), (1, 8)), jnp.float32)
    coefficient = jnp.clip(jnp.exp(math.log(3.0) - 2.3025851 * jax.random.uniform(key_list[2], (2, N), jnp.float32) ** level_of(key_list[2], (2, N), ((1, 8),), -0.2, 0.2)), 0.3, 3.0)
    precond = jnp.clip(jnp.exp(math.log(1.0) - 2.3025851 * jax.random.uniform(key_list[3], (N,), jnp.float32) ** level_of(key_list[3], (N,), ((0, 8),), -0.2, 0.2)), 0.1, 1.0)
    blocks = noise(key_list[4], (2, 7, B, B), (7 * B) ** -0.5, 0.125)
    couplings = draw_couplings(jax.random.fold_in(key_list[8], 71), 0)
    chaos_values = noise(key_list[6], (NNZB, PB, PB), (3 * PB) ** -0.5, 0.875)
    chaos_index = draw_chaos_index(jax.random.fold_in(key_list[8], 71), 0)
    return {"field": field, "right_side": right_side, "coefficient": coefficient, "precond": precond, "blocks": blocks, "couplings": couplings, "chaos_values": chaos_values, "chaos_index": chaos_index}


def stiffness(lowered, blocks, couplings, coefficient, which_term):
    mode_count = lowered.shape[0]
    block_count = lowered.shape[1] // B
    padded = jnp.pad(lowered, ((0, 0), (3 * B, 3 * B)))
    summed = jnp.zeros((mode_count, block_count, B), jnp.float32)
    for offset in range(7):
        window = padded[:, offset * B: offset * B + block_count * B].reshape(mode_count * block_count, B)
        product = jnp.dot(window, blocks[which_term, offset], preferred_element_type=jnp.float32)
        product = product.reshape(mode_count, block_count, B)
        summed = summed + product * couplings[:, offset].astype(jnp.float32)[None, :, None]
    return summed.reshape(mode_count, -1) * coefficient[which_term][None, :]


def chaos_matrix(chaos_values, chaos_index):
    block_ids = jnp.arange(PBLK, dtype=jnp.int32)
    row_hits = (chaos_index[:, 0:1] == block_ids[None, :]).astype(jnp.float32)
    col_hits = (chaos_index[:, 1:2] == block_ids[None, :]).astype(jnp.float32)
    spread_blocks = jnp.einsum("br,bc,bij->ricj", row_hits, col_hits, chaos_values.astype(jnp.float32))
    return spread_blocks.reshape(P_SIZE, P_SIZE).astype(jnp.bfloat16)


def reference(field, right_side, coefficient, precond, blocks, couplings, chaos_values, chaos_index):
    lowered = field.astype(jnp.bfloat16)
    diffused = stiffness(lowered, blocks, couplings, coefficient, 0)
    spread = stiffness(lowered, blocks, couplings, coefficient, 1).astype(jnp.bfloat16)
    matrix = chaos_matrix(chaos_values, chaos_index)
    mixed = jnp.dot(matrix, spread, preferred_element_type=jnp.float32)
    residual = right_side - (diffused + mixed)
    updated = field + precond[None, :] * residual
    return updated, residual
```

```python
import functools

import jax
import jax.numpy as jnp
from jax import lax
from jax.experimental import pallas as pl
from jax.experimental.pallas import tpu as pltpu
from jax.sharding import PartitionSpec as P

MESH = pl.DeviceIdType.MESH
REACH = 3


def kernel(
    modes, slabs, group,
    field, right, coefficient, blocks, couplings, chaos_values, chaos_index,
    out,
    low, fbuf, rbuf, weights, coef, gathered, matrix,
    field_sem, right_sem, weight_sem, coef_sem, out_sem,
    halo_send, halo_recv, near_send, far_send, forward_send, recv,
):
    rows, width = field.shape
    size = blocks.shape[-1]
    count = width // size
    groups = count // group
    span = group * size
    taps = 2 * REACH + 1
    pairs = modes // 2
    me = lax.axis_index("mode")
    slab = lax.axis_index("mesh")
    sibling = me + 1 - 2 * lax.rem(me, 2)
    peers = [lax.rem(me + 2 * j, modes) for j in range(1, pairs)]
    has_left = slab > 0
    has_right = slab < slabs - 1

    def columns(g):
        return pl.ds(pl.multiple_of(g * span, span), span)

    def field_copy(g):
        return pltpu.make_async_copy(field.at[:, columns(g)], fbuf.at[:, columns(g)], field_sem.at[g])

    def right_copy(g):
        return pltpu.make_async_copy(right.at[:, columns(g)], rbuf.at[:, columns(g)], right_sem.at[g])

    def weight_copy(k):
        return pltpu.make_async_copy(blocks.at[k], weights.at[k], weight_sem.at[k])

    def out_copy(g):
        return pltpu.make_async_copy(rbuf.at[:, columns(g)], out.at[:, columns(g)], out_sem.at[g])

    field_copy(0).start()
    field_copy(groups - 1).start()
    weight_copy(1).start()
    coef_copy = pltpu.make_async_copy(coefficient, coef, coef_sem)
    coef_copy.start()

    @pl.loop(1, groups - 1)
    def _(g):
        field_copy(g).start()

    weight_copy(0).start()

    @pl.loop(0, groups)
    def _(g):
        right_copy(g).start()

    barrier = pltpu.get_barrier_semaphore()
    for other in [sibling] + peers:
        pl.semaphore_signal(barrier, inc=1, device_id={"mode": other}, device_id_type=MESH)

    @pl.when(has_left)
    def _():
        pl.semaphore_signal(barrier, inc=1, device_id={"mesh": slab - 1}, device_id_type=MESH)

    @pl.when(has_right)
    def _():
        pl.semaphore_signal(barrier, inc=1, device_id={"mesh": slab + 1}, device_id_type=MESH)

    def lower(g):
        for b in range(group):
            at = g * group + b
            cols = pl.ds(pl.multiple_of(at * size, size), size)
            low[REACH + at] = fbuf[:, cols].astype(jnp.bfloat16)

    field_copy(0).wait()
    lower(0)
    field_copy(groups - 1).wait()
    lower(groups - 1)

    pl.semaphore_wait(barrier, pairs + jnp.minimum(slab, 1) + jnp.minimum(slabs - 1 - slab, 1))

    to_left = pltpu.make_async_remote_copy(
        src_ref=low.at[pl.ds(REACH, REACH)], dst_ref=low.at[pl.ds(REACH + count, REACH)],
        send_sem=halo_send.at[0], recv_sem=halo_recv.at[0],
        device_id={"mesh": slab - 1}, device_id_type=MESH)
    to_right = pltpu.make_async_remote_copy(
        src_ref=low.at[pl.ds(count, REACH)], dst_ref=low.at[pl.ds(0, REACH)],
        send_sem=halo_send.at[1], recv_sem=halo_recv.at[1],
        device_id={"mesh": slab + 1}, device_id_type=MESH)

    @pl.when(has_left)
    def _():
        to_left.start()

    @pl.when(has_right)
    def _():
        to_right.start()

    @pl.when(jnp.logical_not(has_left))
    def _():
        low[pl.ds(0, REACH)] = jnp.zeros((REACH, rows, size), jnp.bfloat16)

    @pl.when(jnp.logical_not(has_right))
    def _():
        low[pl.ds(REACH + count, REACH)] = jnp.zeros((REACH, rows, size), jnp.bfloat16)

    field_copy(1).wait()
    lower(1)
    weight_copy(1).wait()
    coef_copy.wait()

    def stencil(g, k):
        tall = []
        for b in range(group):
            at = g * group + b
            wide = []
            for c in range(taps):
                keep = jnp.full((rows, size), couplings[c, at].astype(jnp.float32)).astype(jnp.bfloat16)
                wide.append(low[at + c] * keep)
            tall.append(jnp.concatenate(wide, axis=1))
        stacked = jnp.concatenate(tall, axis=0)
        return jnp.dot(stacked, weights[k].reshape(taps * size, size), preferred_element_type=jnp.float32)

    def piece(slot, g):
        return gathered.at[slot, pl.ds(g * group, group)]

    def send(slot, g, target, sem):
        return pltpu.make_async_remote_copy(
            src_ref=piece(slot, g), dst_ref=piece(slot, g), send_sem=sem, recv_sem=recv.at[slot, g],
            device_id={"mode": target}, device_id_type=MESH)

    def turn(t):
        return lax.rem(t + 1, groups)

    @pl.loop(0, groups)
    def _(t):
        g = turn(t)

        @pl.when(t + 2 <= groups - 2)
        def _():
            field_copy(t + 2).wait()
            lower(t + 2)

        @pl.when(jnp.logical_and(t == groups - 2, has_right))
        def _():
            to_left.wait_recv()

        @pl.when(jnp.logical_and(t == groups - 1, has_left))
        def _():
            to_right.wait_recv()

        sums = stencil(g, 1)
        for b in range(group):
            at = g * group + b
            cols = pl.ds(pl.multiple_of(at * size, size), size)
            scaled = sums[b * rows:(b + 1) * rows] * coef[1:2, cols]
            gathered[me, at] = scaled.astype(jnp.bfloat16)
        for j, peer in enumerate(peers):
            send(me, g, peer, far_send.at[j, g]).start()
        send(me, g, sibling, near_send.at[g]).start()

    part = chaos_values.shape[1]
    parts = modes * rows // part
    lane_of = lax.broadcasted_iota(jnp.int32, (part, modes * rows), 1)
    row_of = lax.broadcasted_iota(jnp.int32, (part, modes * rows), 0)
    repeat = (lax.rem(lane_of, part) == row_of).astype(jnp.float32).astype(jnp.bfloat16)
    block_of = lane_of // part
    links = chaos_values.shape[0] // parts
    for q in range(rows // part):
        total = jnp.zeros((part, modes * rows), jnp.float32)
        for e in range(links):
            at = (me * (rows // part) + q) * links + e
            spread_out = jnp.dot(chaos_values[at], repeat, preferred_element_type=jnp.float32)
            total = total + jnp.where(block_of == chaos_index[1, at], spread_out, 0.0)
        matrix[q * part:(q + 1) * part, :] = total.astype(jnp.bfloat16)

    weight_copy(0).wait()

    @pl.loop(0, groups)
    def _(t):
        g = turn(t)
        right_copy(g).wait()
        sums = stencil(g, 0)
        for b in range(group):
            at = g * group + b
            cols = pl.ds(pl.multiple_of(at * size, size), size)
            rbuf[:, cols] = rbuf[:, cols] - sums[b * rows:(b + 1) * rows] * coef[0:1, cols]

    def mix(g):
        send(sibling, g, sibling, near_send.at[g]).wait_recv()
        for j, peer in enumerate(peers):
            other = peer + 1 - 2 * lax.rem(peer, 2)
            send(other, g, sibling, forward_send.at[j, g]).wait_recv()
        for b in range(group):
            at = g * group + b
            cols = pl.ds(pl.multiple_of(at * size, size), size)
            mixed = jnp.dot(
                matrix[...], gathered[:, at].reshape(modes * rows, size), preferred_element_type=jnp.float32)
            rbuf[:, cols] = rbuf[:, cols] - mixed
        out_copy(g).start()

    def forward(g):
        for j, peer in enumerate(peers):
            send(peer, g, peer, far_send.at[j, g]).wait_recv()
            send(peer, g, sibling, forward_send.at[j, g]).start()

    forward(turn(0))

    @pl.loop(1, groups)
    def _(t):
        forward(turn(t))
        mix(turn(t - 1))

    mix(turn(groups - 1))

    @pl.loop(0, groups)
    def _(g):
        send(me, g, sibling, near_send.at[g]).wait_send()
        for j, peer in enumerate(peers):
            send(me, g, peer, far_send.at[j, g]).wait_send()
            send(peer, g, sibling, forward_send.at[j, g]).wait_send()
        out_copy(g).wait()

    @pl.when(has_left)
    def _():
        to_left.wait_send()

    @pl.when(has_right)
    def _():
        to_right.wait_send()


def finish_kernel(field, found, precond, updated, residual):
    value = found[...]
    residual[...] = value
    updated[...] = field[...] + precond[...] * value


def shards(modes, slabs, field, right_side, coefficient, precond, blocks, couplings, chaos_values, chaos_index):
    rows, width = field.shape
    size = blocks.shape[-1]
    taps = blocks.shape[1]
    count = width // size
    group = 4
    groups = count // group
    others = max(modes // 2 - 1, 1)
    anywhere = pl.BlockSpec(memory_space=pl.ANY)
    scalars = pl.BlockSpec(memory_space=pltpu.SMEM)
    dma = pltpu.SemaphoreType.DMA
    found = pl.pallas_call(
        functools.partial(kernel, modes, slabs, group),
        out_shape=jax.ShapeDtypeStruct((rows, width), jnp.float32),
        in_specs=[anywhere, anywhere, anywhere, anywhere, scalars, pl.BlockSpec(memory_space=pltpu.VMEM), scalars],
        out_specs=anywhere,
        scratch_shapes=[
            pltpu.VMEM((count + 2 * REACH, rows, size), jnp.bfloat16),
            pltpu.VMEM((rows, width), jnp.float32),
            pltpu.VMEM((rows, width), jnp.float32),
            pltpu.VMEM(blocks.shape, jnp.bfloat16),
            pltpu.VMEM(coefficient.shape, jnp.float32),
            pltpu.VMEM((modes, count, rows, size), jnp.bfloat16),
            pltpu.VMEM((rows, modes * rows), jnp.bfloat16),
            dma((groups,)), dma((groups,)), dma((2,)), dma, dma((groups,)),
            dma((2,)), dma((2,)), dma((groups,)), dma((others, groups)), dma((others, groups)),
            dma((modes, groups)),
        ],
        compiler_params=pltpu.CompilerParams(
            collective_id=0, has_side_effects=True, vmem_limit_bytes=56 * 1024 * 1024),
        name="gather_mix",
    )(field, right_side, coefficient, blocks, couplings.T, chaos_values, chaos_index.T)
    step = min(2048, width)
    tile = pl.BlockSpec((rows, step), lambda i: (0, i))
    return pl.pallas_call(
        finish_kernel,
        grid=(width // step,),
        out_shape=[jax.ShapeDtypeStruct((rows, width), jnp.float32)] * 2,
        in_specs=[tile, tile, pl.BlockSpec((1, step), lambda i: (0, i))],
        out_specs=[tile, tile],
        name="finish",
    )(field, found, precond[None, :])


def solution(mesh):
    placed = (
        P("mode", "mesh"),
        P("mode", "mesh"),
        P(None, "mesh"),
        P("mesh"),
        P(),
        P("mesh", None),
        P(),
        P(),
    )
    return jax.shard_map(
        functools.partial(shards, mesh.shape["mode"], mesh.shape["mesh"]),
        mesh=mesh,
        in_specs=placed,
        out_specs=(P("mode", "mesh"), P("mode", "mesh")),
        check_vma=False,
    )
```

```python
import functools

import jax
import jax.numpy as jnp
from jax import lax
from jax.experimental import pallas as pl
from jax.experimental.pallas import tpu as pltpu
from jax.sharding import PartitionSpec as P

MESH = pl.DeviceIdType.MESH
REACH = 3


def kernel(
    modes, slabs, group,
    field, right, coefficient, blocks, couplings, chaos_values, chaos_index,
    fbuf, rbuf,
    low, weights, coef, gathered, matrix, hits,
    field_sem, right_sem, weight_sem, coef_sem,
    halo_send, halo_recv, near_send, far_send, forward_send, recv,
):
    rows, width = field.shape
    size = blocks.shape[-1]
    count = width // size
    groups = count // group
    span = group * size
    taps = 2 * REACH + 1
    pairs = modes // 2
    me = lax.axis_index("mode")
    slab = lax.axis_index("mesh")
    sibling = me + 1 - 2 * lax.rem(me, 2)
    peers = [lax.rem(me + 2 * j, modes) for j in range(1, pairs)]
    has_left = slab > 0
    has_right = slab < slabs - 1

    def columns(g):
        return pl.ds(pl.multiple_of(g * span, span), span)

    def field_copy(g):
        return pltpu.make_async_copy(field.at[:, columns(g)], fbuf.at[:, columns(g)], field_sem.at[g])

    def right_copy(g):
        return pltpu.make_async_copy(right.at[:, columns(g)], rbuf.at[:, columns(g)], right_sem.at[g])

    def weight_copy(k):
        return pltpu.make_async_copy(blocks.at[k], weights.at[k], weight_sem.at[k])

    field_copy(0).start()
    field_copy(groups - 1).start()
    weight_copy(1).start()
    coef_copy = pltpu.make_async_copy(coefficient, coef, coef_sem)
    coef_copy.start()

    @pl.loop(1, groups - 1)
    def _(g):
        field_copy(g).start()

    weight_copy(0).start()

    @pl.loop(0, groups)
    def _(g):
        right_copy(g).start()

    barrier = pltpu.get_barrier_semaphore()
    for other in [sibling] + peers:
        pl.semaphore_signal(barrier, inc=1, device_id={"mode": other}, device_id_type=MESH)

    @pl.when(has_left)
    def _():
        pl.semaphore_signal(barrier, inc=1, device_id={"mesh": slab - 1}, device_id_type=MESH)

    @pl.when(has_right)
    def _():
        pl.semaphore_signal(barrier, inc=1, device_id={"mesh": slab + 1}, device_id_type=MESH)

    def lower(g):
        for b in range(group):
            at = g * group + b
            cols = pl.ds(pl.multiple_of(at * size, size), size)
            low[REACH + at] = fbuf[:, cols].astype(jnp.bfloat16)

    field_copy(0).wait()
    lower(0)
    field_copy(groups - 1).wait()
    lower(groups - 1)

    pl.semaphore_wait(barrier, pairs + jnp.minimum(slab, 1) + jnp.minimum(slabs - 1 - slab, 1))

    to_left = pltpu.make_async_remote_copy(
        src_ref=low.at[pl.ds(REACH, REACH)], dst_ref=low.at[pl.ds(REACH + count, REACH)],
        send_sem=halo_send.at[0], recv_sem=halo_recv.at[0],
        device_id={"mesh": slab - 1}, device_id_type=MESH)
    to_right = pltpu.make_async_remote_copy(
        src_ref=low.at[pl.ds(count, REACH)], dst_ref=low.at[pl.ds(0, REACH)],
        send_sem=halo_send.at[1], recv_sem=halo_recv.at[1],
        device_id={"mesh": slab + 1}, device_id_type=MESH)

    @pl.when(has_left)
    def _():
        to_left.start()

    @pl.when(has_right)
    def _():
        to_right.start()

    @pl.when(jnp.logical_not(has_left))
    def _():
        low[pl.ds(0, REACH)] = jnp.zeros((REACH, rows, size), jnp.bfloat16)

    @pl.when(jnp.logical_not(has_right))
    def _():
        low[pl.ds(REACH + count, REACH)] = jnp.zeros((REACH, rows, size), jnp.bfloat16)

    field_copy(1).wait()
    lower(1)
    weight_copy(1).wait()
    coef_copy.wait()

    def stencil(g, k):
        tall = []
        for b in range(group):
            at = g * group + b
            wide = []
            for c in range(taps):
                keep = jnp.full((rows, size), couplings[c, at].astype(jnp.float32)).astype(jnp.bfloat16)
                wide.append(low[at + c] * keep)
            tall.append(jnp.concatenate(wide, axis=1))
        stacked = jnp.concatenate(tall, axis=0)
        return jnp.dot(stacked, weights[k].reshape(taps * size, size), preferred_element_type=jnp.float32)

    def piece(slot, g):
        return gathered.at[slot, pl.ds(g * group, group)]

    def send(slot, g, target, sem):
        return pltpu.make_async_remote_copy(
            src_ref=piece(slot, g), dst_ref=piece(slot, g), send_sem=sem, recv_sem=recv.at[slot, g],
            device_id={"mode": target}, device_id_type=MESH)

    def turn(t):
        return lax.rem(t + 1, groups)

    @pl.loop(0, groups)
    def _(t):
        g = turn(t)

        @pl.when(t + 2 <= groups - 2)
        def _():
            field_copy(t + 2).wait()
            lower(t + 2)

        @pl.when(jnp.logical_and(t == groups - 2, has_right))
        def _():
            to_left.wait_recv()

        @pl.when(jnp.logical_and(t == groups - 1, has_left))
        def _():
            to_right.wait_recv()

        sums = stencil(g, 1)
        for b in range(group):
            at = g * group + b
            cols = pl.ds(pl.multiple_of(at * size, size), size)
            scaled = sums[b * rows:(b + 1) * rows] * coef[1:2, cols]
            gathered[me, at] = scaled.astype(jnp.bfloat16)
        for j, peer in enumerate(peers):
            send(me, g, peer, far_send.at[j, g]).start()
        send(me, g, sibling, near_send.at[g]).start()

    part, _, links = chaos_values.shape
    total_rows = modes * rows
    per_row = links * part // total_rows
    column_of = lax.broadcasted_iota(jnp.int32, (1, total_rows), 1) // part
    for n in range(links):
        hits[n:n + 1, :] = (column_of == chaos_index[1, n]).astype(jnp.float32)
    lane_of = lax.broadcasted_iota(jnp.int32, (part, total_rows), 1)
    step_of = lax.broadcasted_iota(jnp.int32, (part, total_rows), 0)
    repeat = (lax.rem(lane_of, part) == step_of).astype(jnp.float32).astype(jnp.bfloat16)
    row_of = lax.broadcasted_iota(jnp.int32, (rows, links), 0)
    owner_of = lax.broadcasted_iota(jnp.int32, (rows, links), 1) // per_row
    owned = owner_of == row_of // part + me * (rows // part)
    built = jnp.zeros((rows, total_rows), jnp.float32)
    for i in range(part):
        spread_out = lax.dot_general(
            chaos_values[i], repeat, (((0,), (0,)), ((), ())), preferred_element_type=jnp.float32)
        placed = (spread_out * hits[...]).astype(jnp.bfloat16)
        mine = jnp.logical_and(owned, lax.rem(row_of, part) == i).astype(jnp.float32).astype(jnp.bfloat16)
        built = built + jnp.dot(mine, placed, preferred_element_type=jnp.float32)
    matrix[...] = built.astype(jnp.bfloat16)

    weight_copy(0).wait()

    @pl.loop(0, groups)
    def _(t):
        g = turn(t)
        right_copy(g).wait()
        sums = stencil(g, 0)
        for b in range(group):
            at = g * group + b
            cols = pl.ds(pl.multiple_of(at * size, size), size)
            rbuf[:, cols] = rbuf[:, cols] - sums[b * rows:(b + 1) * rows] * coef[0:1, cols]

    def mix(g):
        send(sibling, g, sibling, near_send.at[g]).wait_recv()
        for j, peer in enumerate(peers):
            other = peer + 1 - 2 * lax.rem(peer, 2)
            send(other, g, sibling, forward_send.at[j, g]).wait_recv()
        for b in range(group):
            at = g * group + b
            cols = pl.ds(pl.multiple_of(at * size, size), size)
            mixed = jnp.dot(
                matrix[...], gathered[:, at].reshape(modes * rows, size), preferred_element_type=jnp.float32)
            rbuf[:, cols] = rbuf[:, cols] - mixed

    def forward(g):
        for j, peer in enumerate(peers):
            send(peer, g, peer, far_send.at[j, g]).wait_recv()
            send(peer, g, sibling, forward_send.at[j, g]).start()

    forward(turn(0))

    @pl.loop(1, groups)
    def _(t):
        forward(turn(t))
        mix(turn(t - 1))

    mix(turn(groups - 1))

    @pl.loop(0, groups)
    def _(g):
        send(me, g, sibling, near_send.at[g]).wait_send()
        for j, peer in enumerate(peers):
            send(me, g, peer, far_send.at[j, g]).wait_send()
            send(peer, g, sibling, forward_send.at[j, g]).wait_send()

    @pl.when(has_left)
    def _():
        to_left.wait_send()

    @pl.when(has_right)
    def _():
        to_right.wait_send()


def finish_kernel(pieces, field, found, precond, updated, residual, stage, sems):
    rows, width = field.shape
    span = width // pieces

    def columns(i):
        return pl.ds(pl.multiple_of(i * span, span), span)

    def found_copy(i):
        return pltpu.make_async_copy(found.at[:, columns(i)], residual.at[:, columns(i)], sems.at[0, i])

    def stage_copy(i):
        return pltpu.make_async_copy(stage.at[:, columns(i)], updated.at[:, columns(i)], sems.at[1, i])

    @pl.loop(0, pieces)
    def _(i):
        found_copy(i).start()
        cols = columns(i)
        stage[:, cols] = field[:, cols] + precond[:, cols] * found[:, cols]
        stage_copy(i).start()

    @pl.loop(0, pieces)
    def _(i):
        found_copy(i).wait()
        stage_copy(i).wait()


def shards(modes, slabs, field, right_side, coefficient, precond, blocks, couplings, chaos_values, chaos_index):
    rows, width = field.shape
    size = blocks.shape[-1]
    taps = blocks.shape[1]
    count = width // size
    group = 4
    groups = count // group
    others = max(modes // 2 - 1, 1)
    inside = pl.BlockSpec(memory_space=pltpu.VMEM)
    anywhere = pl.BlockSpec(memory_space=pl.ANY)
    spare = 67043328 - 2 * rows * width * 4 - 96 * 1024
    scalars = pl.BlockSpec(memory_space=pltpu.SMEM)
    dma = pltpu.SemaphoreType.DMA
    kept, found = pl.pallas_call(
        functools.partial(kernel, modes, slabs, group),
        out_shape=[pltpu.VMEM((rows, width), jnp.float32)] * 2,
        in_specs=[anywhere, anywhere, anywhere, anywhere, scalars, pl.BlockSpec(memory_space=pltpu.VMEM), scalars],
        out_specs=[inside] * 2,
        scratch_shapes=[
            pltpu.VMEM((count + 2 * REACH, rows, size), jnp.bfloat16),
            pltpu.VMEM(blocks.shape, jnp.bfloat16),
            pltpu.VMEM(coefficient.shape, jnp.float32),
            pltpu.VMEM((modes, count, rows, size), jnp.bfloat16),
            pltpu.VMEM((rows, modes * rows), jnp.bfloat16),
            pltpu.VMEM((chaos_values.shape[0], modes * rows), jnp.float32),
            dma((groups,)), dma((groups,)), dma((2,)), dma,
            dma((2,)), dma((2,)), dma((groups,)), dma((others, groups)), dma((others, groups)),
            dma((modes, groups)),
        ],
        compiler_params=pltpu.CompilerParams(
            collective_id=0, has_side_effects=True, vmem_limit_bytes=spare),
        name="gather_mix",
    )(field, right_side, coefficient, blocks, couplings.T, chaos_values.transpose(1, 2, 0), chaos_index.T)
    pieces = 16
    return pl.pallas_call(
        functools.partial(finish_kernel, pieces),
        out_shape=[jax.ShapeDtypeStruct((rows, width), jnp.float32)] * 2,
        in_specs=[inside] * 3,
        out_specs=[anywhere] * 2,
        scratch_shapes=[pltpu.VMEM((rows, width), jnp.float32), dma((2, pieces))],
        compiler_params=pltpu.CompilerParams(vmem_limit_bytes=8 * 1024 * 1024),
        name="finish",
    )(kept, found, precond[None, :])


def solution(mesh):
    placed = (
        P("mode", "mesh"),
        P("mode", "mesh"),
        P(None, "mesh"),
        P("mesh"),
        P(),
        P("mesh", None),
        P(),
        P(),
    )
    return jax.shard_map(
        functools.partial(shards, mesh.shape["mode"], mesh.shape["mesh"]),
        mesh=mesh,
        in_specs=placed,
        out_specs=(P("mode", "mesh"), P("mode", "mesh")),
        check_vma=False,
    )
```

```python
import functools

import jax
import jax.numpy as jnp
from jax import lax
from jax.experimental import pallas as pl
from jax.experimental.pallas import tpu as pltpu
from jax.sharding import PartitionSpec as P

MESH = pl.DeviceIdType.MESH
REACH = 3


def kernel(
    modes, slabs, group,
    field, right, coefficient, blocks, couplings, chaos_values, chaos_index,
    fbuf, rbuf,
    low, weights, coef, gathered, matrix, hits,
    field_sem, right_sem, weight_sem, coef_sem,
    halo_send, halo_recv, near_send, far_send, forward_send, recv,
):
    rows, width = field.shape
    size = blocks.shape[-1]
    count = width // size
    groups = count // group
    span = group * size
    taps = 2 * REACH + 1
    pairs = modes // 2
    me = lax.axis_index("mode")
    slab = lax.axis_index("mesh")
    sibling = me + 1 - 2 * lax.rem(me, 2)
    peers = [lax.rem(me + 2 * j, modes) for j in range(1, pairs)]
    has_left = slab > 0
    has_right = slab < slabs - 1

    def columns(g):
        return pl.ds(pl.multiple_of(g * span, span), span)

    def field_copy(g):
        return pltpu.make_async_copy(field.at[:, columns(g)], fbuf.at[:, columns(g)], field_sem.at[g])

    def right_copy(g):
        return pltpu.make_async_copy(right.at[:, columns(g)], rbuf.at[:, columns(g)], right_sem.at[g])

    def weight_copy(k):
        return pltpu.make_async_copy(blocks.at[k], weights.at[k], weight_sem.at[k])

    field_copy(0).start()
    field_copy(groups - 1).start()
    weight_copy(1).start()
    coef_copy = pltpu.make_async_copy(coefficient, coef, coef_sem)
    coef_copy.start()

    @pl.loop(1, groups - 1)
    def _(g):
        field_copy(g).start()

    weight_copy(0).start()

    @pl.loop(0, groups)
    def _(g):
        right_copy(g).start()

    barrier = pltpu.get_barrier_semaphore()
    for other in [sibling] + peers:
        pl.semaphore_signal(barrier, inc=1, device_id={"mode": other}, device_id_type=MESH)

    @pl.when(has_left)
    def _():
        pl.semaphore_signal(barrier, inc=1, device_id={"mesh": slab - 1}, device_id_type=MESH)

    @pl.when(has_right)
    def _():
        pl.semaphore_signal(barrier, inc=1, device_id={"mesh": slab + 1}, device_id_type=MESH)

    def lower(g):
        for b in range(group):
            at = g * group + b
            cols = pl.ds(pl.multiple_of(at * size, size), size)
            low[REACH + at] = fbuf[:, cols].astype(jnp.bfloat16)

    field_copy(0).wait()
    lower(0)
    field_copy(groups - 1).wait()
    lower(groups - 1)

    pl.semaphore_wait(barrier, pairs + jnp.minimum(slab, 1) + jnp.minimum(slabs - 1 - slab, 1))

    to_left = pltpu.make_async_remote_copy(
        src_ref=low.at[pl.ds(REACH, REACH)], dst_ref=low.at[pl.ds(REACH + count, REACH)],
        send_sem=halo_send.at[0], recv_sem=halo_recv.at[0],
        device_id={"mesh": slab - 1}, device_id_type=MESH)
    to_right = pltpu.make_async_remote_copy(
        src_ref=low.at[pl.ds(count, REACH)], dst_ref=low.at[pl.ds(0, REACH)],
        send_sem=halo_send.at[1], recv_sem=halo_recv.at[1],
        device_id={"mesh": slab + 1}, device_id_type=MESH)

    @pl.when(has_left)
    def _():
        to_left.start()

    @pl.when(has_right)
    def _():
        to_right.start()

    @pl.when(jnp.logical_not(has_left))
    def _():
        low[pl.ds(0, REACH)] = jnp.zeros((REACH, rows, size), jnp.bfloat16)

    @pl.when(jnp.logical_not(has_right))
    def _():
        low[pl.ds(REACH + count, REACH)] = jnp.zeros((REACH, rows, size), jnp.bfloat16)

    field_copy(1).wait()
    lower(1)
    weight_copy(1).wait()
    coef_copy.wait()

    def stencil(g, k):
        tall = []
        for b in range(group):
            at = g * group + b
            wide = []
            for c in range(taps):
                keep = jnp.full((rows, size), couplings[c, at].astype(jnp.float32)).astype(jnp.bfloat16)
                wide.append(low[at + c] * keep)
            tall.append(jnp.concatenate(wide, axis=1))
        stacked = jnp.concatenate(tall, axis=0)
        return jnp.dot(stacked, weights[k].reshape(taps * size, size), preferred_element_type=jnp.float32)

    def piece(slot, g):
        return gathered.at[slot, pl.ds(g * group, group)]

    def send(slot, g, target, sem):
        return pltpu.make_async_remote_copy(
            src_ref=piece(slot, g), dst_ref=piece(slot, g), send_sem=sem, recv_sem=recv.at[slot, g],
            device_id={"mode": target}, device_id_type=MESH)

    def turn(t):
        return lax.rem(t + 1, groups)

    @pl.loop(0, groups)
    def _(t):
        g = turn(t)

        @pl.when(t + 2 <= groups - 2)
        def _():
            field_copy(t + 2).wait()
            lower(t + 2)

        @pl.when(jnp.logical_and(t == groups - 2, has_right))
        def _():
            to_left.wait_recv()

        @pl.when(jnp.logical_and(t == groups - 1, has_left))
        def _():
            to_right.wait_recv()

        sums = stencil(g, 1)
        for b in range(group):
            at = g * group + b
            cols = pl.ds(pl.multiple_of(at * size, size), size)
            scaled = sums[b * rows:(b + 1) * rows] * coef[1:2, cols]
            gathered[me, at] = scaled.astype(jnp.bfloat16)
        for j, peer in enumerate(peers):
            send(me, g, peer, far_send.at[j, g]).start()
        send(me, g, sibling, near_send.at[g]).start()

    part, _, links = chaos_values.shape
    total_rows = modes * rows
    per_row = links * part // total_rows
    column_of = lax.broadcasted_iota(jnp.int32, (1, total_rows), 1) // part
    for n in range(links):
        hits[n:n + 1, :] = (column_of == chaos_index[1, n]).astype(jnp.float32)
    lane_of = lax.broadcasted_iota(jnp.int32, (part, total_rows), 1)
    step_of = lax.broadcasted_iota(jnp.int32, (part, total_rows), 0)
    repeat = (lax.rem(lane_of, part) == step_of).astype(jnp.float32).astype(jnp.bfloat16)
    row_of = lax.broadcasted_iota(jnp.int32, (rows, links), 0)
    owner_of = lax.broadcasted_iota(jnp.int32, (rows, links), 1) // per_row
    owned = owner_of == row_of // part + me * (rows // part)
    built = jnp.zeros((rows, total_rows), jnp.float32)
    for i in range(part):
        spread_out = lax.dot_general(
            chaos_values[i], repeat, (((0,), (0,)), ((), ())), preferred_element_type=jnp.float32)
        placed = (spread_out * hits[0:links, :]).astype(jnp.bfloat16)
        mine = jnp.logical_and(owned, lax.rem(row_of, part) == i).astype(jnp.float32).astype(jnp.bfloat16)
        built = built + jnp.dot(mine, placed, preferred_element_type=jnp.float32)
    matrix[...] = built.astype(jnp.bfloat16)

    weight_copy(0).wait()

    @pl.loop(0, groups)
    def _(t):
        g = turn(t)
        right_copy(g).wait()
        sums = stencil(g, 0)
        for b in range(group):
            at = g * group + b
            cols = pl.ds(pl.multiple_of(at * size, size), size)
            rbuf[:, cols] = rbuf[:, cols] - sums[b * rows:(b + 1) * rows] * coef[0:1, cols]

    def mix(g):
        send(sibling, g, sibling, near_send.at[g]).wait_recv()
        for j, peer in enumerate(peers):
            other = peer + 1 - 2 * lax.rem(peer, 2)
            send(other, g, sibling, forward_send.at[j, g]).wait_recv()
        for b in range(group):
            at = g * group + b
            cols = pl.ds(pl.multiple_of(at * size, size), size)
            mixed = jnp.dot(
                matrix[...], gathered[:, at].reshape(modes * rows, size), preferred_element_type=jnp.float32)
            rbuf[:, cols] = rbuf[:, cols] - mixed

    def forward(g):
        for j, peer in enumerate(peers):
            send(peer, g, peer, far_send.at[j, g]).wait_recv()
            send(peer, g, sibling, forward_send.at[j, g]).start()

    forward(turn(0))

    @pl.loop(1, groups)
    def _(t):
        forward(turn(t))
        mix(turn(t - 1))

    mix(turn(groups - 1))

    @pl.loop(0, groups)
    def _(g):
        send(me, g, sibling, near_send.at[g]).wait_send()
        for j, peer in enumerate(peers):
            send(me, g, peer, far_send.at[j, g]).wait_send()
            send(peer, g, sibling, forward_send.at[j, g]).wait_send()

    @pl.when(has_left)
    def _():
        to_left.wait_send()

    @pl.when(has_right)
    def _():
        to_right.wait_send()


def packed_kernel(
    modes, slabs, group, packed,
    field, right, coefficient, blocks, couplings, chaos_values, chaos_index,
    fbuf, rbuf,
    low, weights, coef, gathered, outgoing, arrived, matrix, hits, picks,
    field_sem, right_sem, weight_sem, coef_sem,
    halo_send, halo_recv, near_send, near_recv, far_send, far_recv, forward_send, forward_recv,
):
    rows, width = field.shape
    size = blocks.shape[-1]
    count = width // size
    groups = count // group
    span = group * size
    taps = 2 * REACH + 1
    pairs = modes // 2
    me = lax.axis_index("mode")
    slab = lax.axis_index("mesh")
    sibling = me + 1 - 2 * lax.rem(me, 2)
    peer = lax.rem(me + 2, modes)
    peers = [peer]
    core = lax.rem(me, 2)
    here = me // 2
    there = peer // 2
    share = group // 2
    has_left = slab > 0
    has_right = slab < slabs - 1

    def columns(g):
        return pl.ds(pl.multiple_of(g * span, span), span)

    def field_copy(g):
        return pltpu.make_async_copy(field.at[:, columns(g)], fbuf.at[:, columns(g)], field_sem.at[g])

    def right_copy(g):
        return pltpu.make_async_copy(right.at[:, columns(g)], rbuf.at[:, columns(g)], right_sem.at[g])

    def weight_copy(k):
        return pltpu.make_async_copy(blocks.at[k], weights.at[k], weight_sem.at[k])

    field_copy(0).start()
    field_copy(groups - 1).start()
    weight_copy(1).start()
    coef_copy = pltpu.make_async_copy(coefficient, coef, coef_sem)
    coef_copy.start()

    @pl.loop(1, groups - 1)
    def _(g):
        field_copy(g).start()

    weight_copy(0).start()

    @pl.loop(0, groups)
    def _(g):
        right_copy(g).start()

    barrier = pltpu.get_barrier_semaphore()
    for other in [sibling] + peers:
        pl.semaphore_signal(barrier, inc=1, device_id={"mode": other}, device_id_type=MESH)

    @pl.when(has_left)
    def _():
        pl.semaphore_signal(barrier, inc=1, device_id={"mesh": slab - 1}, device_id_type=MESH)

    @pl.when(has_right)
    def _():
        pl.semaphore_signal(barrier, inc=1, device_id={"mesh": slab + 1}, device_id_type=MESH)

    def lower(g):
        for b in range(group):
            at = g * group + b
            cols = pl.ds(pl.multiple_of(at * size, size), size)
            low[REACH + at] = fbuf[:, cols].astype(jnp.bfloat16)

    part, _, links = chaos_values.shape
    total_rows = modes * rows
    per_row = links * part // total_rows
    column_of = lax.broadcasted_iota(jnp.int32, (1, total_rows), 1) // part
    for n in range(links):
        hits[n:n + 1, :] = (column_of == chaos_index[1, n]).astype(jnp.float32)
    both = 2 * rows
    tall = packed * part
    lanes = lax.broadcasted_iota(jnp.int32, (1, total_rows), 1)
    pair_of_entry = lax.broadcasted_iota(jnp.int32, (links, total_rows), 0) // per_row * part // both
    earlier = jnp.logical_and(
        lax.broadcasted_iota(jnp.int32, (total_rows, total_rows), 0) // part
        < lax.broadcasted_iota(jnp.int32, (total_rows, total_rows), 1) // part,
        jnp.logical_and(
            lax.broadcasted_iota(jnp.int32, (total_rows, total_rows), 0) // both
            == lax.broadcasted_iota(jnp.int32, (total_rows, total_rows), 1) // both,
            lax.rem(lax.broadcasted_iota(jnp.int32, (total_rows, total_rows), 0), part) == 0))
    earlier = earlier.astype(jnp.float32).astype(jnp.bfloat16)

    def picked(source, target):
        wanted = jnp.max(jnp.where(pair_of_entry == target, hits[0:links, :], 0.0), axis=0, keepdims=True)
        wanted = jnp.where(lanes // both == source, wanted, 0.0)
        before = jnp.dot(
            jnp.broadcast_to(wanted, (8, total_rows)).astype(jnp.bfloat16), earlier,
            preferred_element_type=jnp.float32)[0:1]
        place = before * part + lax.rem(lanes, part).astype(jnp.float32)
        row = lax.broadcasted_iota(jnp.int32, (tall, total_rows), 0).astype(jnp.float32)
        return jnp.where(jnp.logical_and(row == place, wanted > 0.0), 1.0, 0.0).astype(jnp.bfloat16)

    picks[...] = picked(here, there)

    field_copy(0).wait()
    lower(0)
    field_copy(groups - 1).wait()
    lower(groups - 1)

    pl.semaphore_wait(barrier, pairs + jnp.minimum(slab, 1) + jnp.minimum(slabs - 1 - slab, 1))

    to_left = pltpu.make_async_remote_copy(
        src_ref=low.at[pl.ds(REACH, REACH)], dst_ref=low.at[pl.ds(REACH + count, REACH)],
        send_sem=halo_send.at[0], recv_sem=halo_recv.at[0],
        device_id={"mesh": slab - 1}, device_id_type=MESH)
    to_right = pltpu.make_async_remote_copy(
        src_ref=low.at[pl.ds(count, REACH)], dst_ref=low.at[pl.ds(0, REACH)],
        send_sem=halo_send.at[1], recv_sem=halo_recv.at[1],
        device_id={"mesh": slab + 1}, device_id_type=MESH)

    @pl.when(has_left)
    def _():
        to_left.start()

    @pl.when(has_right)
    def _():
        to_right.start()

    @pl.when(jnp.logical_not(has_left))
    def _():
        low[pl.ds(0, REACH)] = jnp.zeros((REACH, rows, size), jnp.bfloat16)

    @pl.when(jnp.logical_not(has_right))
    def _():
        low[pl.ds(REACH + count, REACH)] = jnp.zeros((REACH, rows, size), jnp.bfloat16)

    field_copy(1).wait()
    lower(1)
    weight_copy(1).wait()
    coef_copy.wait()

    def stencil(g, k):
        tall = []
        for b in range(group):
            at = g * group + b
            wide = []
            for c in range(taps):
                keep = jnp.full((rows, size), couplings[c, at].astype(jnp.float32)).astype(jnp.bfloat16)
                wide.append(low[at + c] * keep)
            tall.append(jnp.concatenate(wide, axis=1))
        stacked = jnp.concatenate(tall, axis=0)
        return jnp.dot(stacked, weights[k].reshape(taps * size, size), preferred_element_type=jnp.float32)

    def near(g):
        held = gathered.at[core, pl.ds(g * group, group)]
        return pltpu.make_async_remote_copy(
            src_ref=held, dst_ref=held, send_sem=near_send.at[g], recv_sem=near_recv.at[g],
            device_id={"mode": sibling}, device_id_type=MESH)

    def far(g):
        return pltpu.make_async_remote_copy(
            src_ref=outgoing.at[pl.ds(g * share, share)],
            dst_ref=arrived.at[pl.ds(g * group + core * share, share)],
            send_sem=far_send.at[g], recv_sem=far_recv.at[g],
            device_id={"mode": peer}, device_id_type=MESH)

    def relay(g):
        held = arrived.at[pl.ds(g * group + core * share, share)]
        return pltpu.make_async_remote_copy(
            src_ref=held, dst_ref=held, send_sem=forward_send.at[g], recv_sem=forward_recv.at[g],
            device_id={"mode": sibling}, device_id_type=MESH)

    def pack(g):
        near(g).wait_recv()
        chosen = picks[:, pl.ds(pl.multiple_of(here * both, both), both)]
        for b in range(share):
            at = g * group + core * share + b
            outgoing[g * share + b] = jnp.dot(
                chosen, gathered[:, at].reshape(both, size),
                preferred_element_type=jnp.float32).astype(jnp.bfloat16)
        far(g).start()

    def turn(t):
        return lax.rem(t + 1, groups)

    @pl.loop(0, groups)
    def _(t):
        g = turn(t)

        @pl.when(t + 2 <= groups - 2)
        def _():
            field_copy(t + 2).wait()
            lower(t + 2)

        @pl.when(jnp.logical_and(t == groups - 2, has_right))
        def _():
            to_left.wait_recv()

        @pl.when(jnp.logical_and(t == groups - 1, has_left))
        def _():
            to_right.wait_recv()

        sums = stencil(g, 1)
        for b in range(group):
            at = g * group + b
            cols = pl.ds(pl.multiple_of(at * size, size), size)
            scaled = sums[b * rows:(b + 1) * rows] * coef[1:2, cols]
            gathered[core, at] = scaled.astype(jnp.bfloat16)
        near(g).start()

        @pl.when(t > 0)
        def _():
            pack(turn(t - 1))

    pack(turn(groups - 1))

    lane_of = lax.broadcasted_iota(jnp.int32, (part, total_rows), 1)
    step_of = lax.broadcasted_iota(jnp.int32, (part, total_rows), 0)
    repeat = (lax.rem(lane_of, part) == step_of).astype(jnp.float32).astype(jnp.bfloat16)
    row_of = lax.broadcasted_iota(jnp.int32, (rows, links), 0)
    owner_of = lax.broadcasted_iota(jnp.int32, (rows, links), 1) // per_row
    owned = owner_of == row_of // part + me * (rows // part)
    built = jnp.zeros((rows, total_rows), jnp.float32)
    for i in range(part):
        spread_out = lax.dot_general(
            chaos_values[i], repeat, (((0,), (0,)), ((), ())), preferred_element_type=jnp.float32)
        placed = (spread_out * hits[0:links, :]).astype(jnp.bfloat16)
        mine = jnp.logical_and(owned, lax.rem(row_of, part) == i).astype(jnp.float32).astype(jnp.bfloat16)
        built = built + jnp.dot(mine, placed, preferred_element_type=jnp.float32)
    built = built.astype(jnp.bfloat16)
    matrix[:, both:both + tall] = lax.dot_general(
        built, picked(there, here), (((1,), (1,)), ((), ())),
        preferred_element_type=jnp.float32).astype(jnp.bfloat16)
    hits[0:rows, :] = built.astype(jnp.float32)
    matrix[:, 0:both] = hits[0:rows, pl.ds(pl.multiple_of(here * both, both), both)].astype(jnp.bfloat16)

    weight_copy(0).wait()

    @pl.loop(0, groups)
    def _(t):
        g = turn(t)
        right_copy(g).wait()
        sums = stencil(g, 0)
        for b in range(group):
            at = g * group + b
            cols = pl.ds(pl.multiple_of(at * size, size), size)
            rbuf[:, cols] = rbuf[:, cols] - sums[b * rows:(b + 1) * rows] * coef[0:1, cols]

    def mix(g):
        relay(g).wait_recv()
        for b in range(group):
            at = g * group + b
            cols = pl.ds(pl.multiple_of(at * size, size), size)
            stacked = jnp.concatenate([gathered[:, at].reshape(both, size), arrived[at]], axis=0)
            mixed = jnp.dot(matrix[...], stacked, preferred_element_type=jnp.float32)
            rbuf[:, cols] = rbuf[:, cols] - mixed

    def forward(g):
        far(g).wait_recv()
        relay(g).start()

    forward(turn(0))

    @pl.loop(1, groups)
    def _(t):
        forward(turn(t))
        mix(turn(t - 1))

    mix(turn(groups - 1))

    @pl.loop(0, groups)
    def _(g):
        near(g).wait_send()
        far(g).wait_send()
        relay(g).wait_send()

    @pl.when(has_left)
    def _():
        to_left.wait_send()

    @pl.when(has_right)
    def _():
        to_right.wait_send()


def finish_kernel(pieces, field, found, precond, updated, residual, stage, sems):
    rows, width = field.shape
    span = width // pieces

    def columns(i):
        return pl.ds(pl.multiple_of(i * span, span), span)

    def found_copy(i):
        return pltpu.make_async_copy(found.at[:, columns(i)], residual.at[:, columns(i)], sems.at[0, i])

    def stage_copy(i):
        return pltpu.make_async_copy(stage.at[:, columns(i)], updated.at[:, columns(i)], sems.at[1, i])

    @pl.loop(0, pieces)
    def _(i):
        found_copy(i).start()
        cols = columns(i)
        stage[:, cols] = field[:, cols] + precond[:, cols] * found[:, cols]
        stage_copy(i).start()

    @pl.loop(0, pieces)
    def _(i):
        found_copy(i).wait()
        stage_copy(i).wait()


def choose_kernel(held, fewest, chaos_index, choice):
    entries = chaos_index.shape[1]
    seen = jnp.int32(0)
    for n in range(entries):
        column = chaos_index[1, n]
        crosses = column // held != n * 2 * held // entries // held
        seen = seen | jnp.where(crosses, jnp.int32(1) << column, 0)
    counts = [sum((seen >> (side * held + i)) & 1 for i in range(held)) for side in range(2)]
    choice[0, 0] = jnp.maximum(jnp.maximum(counts[0], counts[1]) - fewest, 0)


def shards(modes, slabs, field, right_side, coefficient, precond, blocks, couplings, chaos_values, chaos_index):
    rows, width = field.shape
    size = blocks.shape[-1]
    taps = blocks.shape[1]
    count = width // size
    group = 4
    groups = count // group
    others = max(modes // 2 - 1, 1)
    inside = pl.BlockSpec(memory_space=pltpu.VMEM)
    anywhere = pl.BlockSpec(memory_space=pl.ANY)
    spare = 67043328 - 2 * rows * width * 4 - 96 * 1024
    scalars = pl.BlockSpec(memory_space=pltpu.SMEM)
    dma = pltpu.SemaphoreType.DMA
    part = chaos_values.shape[1]
    both = 2 * rows
    entries = chaos_values.shape[0]
    common = [
        pltpu.VMEM((count + 2 * REACH, rows, size), jnp.bfloat16),
        pltpu.VMEM(blocks.shape, jnp.bfloat16),
        pltpu.VMEM(coefficient.shape, jnp.float32),
    ]
    waits = [dma((groups,)), dma((groups,)), dma((2,)), dma, dma((2,)), dma((2,))]
    hits = pltpu.VMEM((max(entries, rows), modes * rows), jnp.float32)

    def whole(*operands):
        return run(
            functools.partial(kernel, modes, slabs, group), 0,
            common + [
                pltpu.VMEM((modes, count, rows, size), jnp.bfloat16),
                pltpu.VMEM((rows, modes * rows), jnp.bfloat16),
                hits,
            ] + waits + [dma((groups,)), dma((others, groups)), dma((others, groups)), dma((modes, groups))],
            operands)

    def reduced(packed, *operands):
        tall = packed * part
        return run(
            functools.partial(packed_kernel, modes, slabs, group, packed), packed,
            common + [
                pltpu.VMEM((2, count, rows, size), jnp.bfloat16),
                pltpu.VMEM((count // 2, tall, size), jnp.bfloat16),
                pltpu.VMEM((count, tall, size), jnp.bfloat16),
                pltpu.VMEM((rows, both + tall), jnp.bfloat16),
                hits,
                pltpu.VMEM((tall, modes * rows), jnp.bfloat16),
            ] + waits + [dma((groups,))] * 6,
            operands)

    def run(body, ident, scratch, operands):
        kept, found = pl.pallas_call(
            body,
            out_shape=[pltpu.VMEM((rows, width), jnp.float32)] * 2,
            in_specs=[anywhere, anywhere, anywhere, anywhere, scalars, inside, scalars],
            out_specs=[inside] * 2,
            scratch_shapes=scratch,
            compiler_params=pltpu.CompilerParams(
                collective_id=ident, has_side_effects=True, vmem_limit_bytes=spare),
            name="gather_mix",
        )(*operands[1:])
        pieces = 16
        return tuple(pl.pallas_call(
            functools.partial(finish_kernel, pieces),
            out_shape=[jax.ShapeDtypeStruct((rows, width), jnp.float32)] * 2,
            in_specs=[inside] * 3,
            out_specs=[anywhere] * 2,
            scratch_shapes=[pltpu.VMEM((rows, width), jnp.float32), dma((2, pieces))],
            compiler_params=pltpu.CompilerParams(vmem_limit_bytes=8 * 1024 * 1024),
            name="finish",
        )(kept, found, operands[0]))

    operands = (
        precond[None, :], field, right_side, coefficient, blocks, couplings.T,
        chaos_values.transpose(1, 2, 0), chaos_index.T)
    if modes != 4 or both % part:
        return whole(*operands)
    held = both // part
    fewest = held // 2 + 1
    choice = pl.pallas_call(
        functools.partial(choose_kernel, held, fewest),
        out_shape=jax.ShapeDtypeStruct((1, 1), jnp.int32),
        in_specs=[scalars],
        out_specs=scalars,
        name="choose",
    )(operands[-1])
    return lax.switch(
        choice[0, 0],
        [functools.partial(reduced, packed) for packed in range(fewest, held + 1)],
        *operands)


def solution(mesh):
    placed = (
        P("mode", "mesh"),
        P("mode", "mesh"),
        P(None, "mesh"),
        P("mesh"),
        P(),
        P("mesh", None),
        P(),
        P(),
    )
    return jax.shard_map(
        functools.partial(shards, mesh.shape["mode"], mesh.shape["mesh"]),
        mesh=mesh,
        in_specs=placed,
        out_specs=(P("mode", "mesh"), P("mode", "mesh")),
        check_vma=False,
    )
```

```python
import functools

import jax
import jax.numpy as jnp
from jax import lax
from jax.experimental import pallas as pl
from jax.experimental.pallas import tpu as pltpu
from jax.sharding import PartitionSpec as P

MESH = pl.DeviceIdType.MESH
REACH = 3


def kernel(
    modes, slabs, group,
    field, right, coefficient, blocks, couplings, chaos_values, chaos_index,
    fbuf, rbuf,
    low, weights, coef, gathered, matrix, hits,
    field_sem, right_sem, weight_sem, coef_sem,
    halo_send, halo_recv, near_send, far_send, forward_send, recv,
):
    rows, width = field.shape
    size = blocks.shape[-1]
    count = width // size
    groups = count // group
    span = group * size
    taps = 2 * REACH + 1
    pairs = modes // 2
    me = lax.axis_index("mode")
    slab = lax.axis_index("mesh")
    sibling = me + 1 - 2 * lax.rem(me, 2)
    peers = [lax.rem(me + 2 * j, modes) for j in range(1, pairs)]
    has_left = slab > 0
    has_right = slab < slabs - 1

    def columns(g):
        return pl.ds(pl.multiple_of(g * span, span), span)

    def field_copy(g):
        return pltpu.make_async_copy(field.at[:, columns(g)], fbuf.at[:, columns(g)], field_sem.at[g])

    def right_copy(g):
        return pltpu.make_async_copy(right.at[:, columns(g)], rbuf.at[:, columns(g)], right_sem.at[g])

    def weight_copy(k):
        return pltpu.make_async_copy(blocks.at[k], weights.at[k], weight_sem.at[k])

    field_copy(0).start()
    field_copy(groups - 1).start()
    weight_copy(1).start()
    coef_copy = pltpu.make_async_copy(coefficient, coef, coef_sem)
    coef_copy.start()

    @pl.loop(1, groups - 1)
    def _(g):
        field_copy(g).start()

    weight_copy(0).start()

    @pl.loop(0, groups)
    def _(g):
        right_copy(g).start()

    barrier = pltpu.get_barrier_semaphore()
    for other in [sibling] + peers:
        pl.semaphore_signal(barrier, inc=1, device_id={"mode": other}, device_id_type=MESH)

    @pl.when(has_left)
    def _():
        pl.semaphore_signal(barrier, inc=1, device_id={"mesh": slab - 1}, device_id_type=MESH)

    @pl.when(has_right)
    def _():
        pl.semaphore_signal(barrier, inc=1, device_id={"mesh": slab + 1}, device_id_type=MESH)

    def lower(g):
        for b in range(group):
            at = g * group + b
            cols = pl.ds(pl.multiple_of(at * size, size), size)
            low[REACH + at] = fbuf[:, cols].astype(jnp.bfloat16)

    field_copy(0).wait()
    lower(0)
    field_copy(groups - 1).wait()
    lower(groups - 1)

    pl.semaphore_wait(barrier, pairs + jnp.minimum(slab, 1) + jnp.minimum(slabs - 1 - slab, 1))

    to_left = pltpu.make_async_remote_copy(
        src_ref=low.at[pl.ds(REACH, REACH)], dst_ref=low.at[pl.ds(REACH + count, REACH)],
        send_sem=halo_send.at[0], recv_sem=halo_recv.at[0],
        device_id={"mesh": slab - 1}, device_id_type=MESH)
    to_right = pltpu.make_async_remote_copy(
        src_ref=low.at[pl.ds(count, REACH)], dst_ref=low.at[pl.ds(0, REACH)],
        send_sem=halo_send.at[1], recv_sem=halo_recv.at[1],
        device_id={"mesh": slab + 1}, device_id_type=MESH)

    @pl.when(has_left)
    def _():
        to_left.start()

    @pl.when(has_right)
    def _():
        to_right.start()

    @pl.when(jnp.logical_not(has_left))
    def _():
        low[pl.ds(0, REACH)] = jnp.zeros((REACH, rows, size), jnp.bfloat16)

    @pl.when(jnp.logical_not(has_right))
    def _():
        low[pl.ds(REACH + count, REACH)] = jnp.zeros((REACH, rows, size), jnp.bfloat16)

    field_copy(1).wait()
    lower(1)
    weight_copy(1).wait()
    coef_copy.wait()

    def stencil(g, k):
        tall = []
        for b in range(group):
            at = g * group + b
            wide = []
            for c in range(taps):
                keep = jnp.full((rows, size), couplings[c, at].astype(jnp.float32)).astype(jnp.bfloat16)
                wide.append(low[at + c] * keep)
            tall.append(jnp.concatenate(wide, axis=1))
        stacked = jnp.concatenate(tall, axis=0)
        return jnp.dot(stacked, weights[k].reshape(taps * size, size), preferred_element_type=jnp.float32)

    def piece(slot, g):
        return gathered.at[slot, pl.ds(g * group, group)]

    def send(slot, g, target, sem):
        return pltpu.make_async_remote_copy(
            src_ref=piece(slot, g), dst_ref=piece(slot, g), send_sem=sem, recv_sem=recv.at[slot, g],
            device_id={"mode": target}, device_id_type=MESH)

    def turn(t):
        return lax.rem(t + 1, groups)

    @pl.loop(0, groups)
    def _(t):
        g = turn(t)

        @pl.when(t + 2 <= groups - 2)
        def _():
            field_copy(t + 2).wait()
            lower(t + 2)

        @pl.when(jnp.logical_and(t == groups - 2, has_right))
        def _():
            to_left.wait_recv()

        @pl.when(jnp.logical_and(t == groups - 1, has_left))
        def _():
            to_right.wait_recv()

        sums = stencil(g, 1)
        for b in range(group):
            at = g * group + b
            cols = pl.ds(pl.multiple_of(at * size, size), size)
            scaled = sums[b * rows:(b + 1) * rows] * coef[1:2, cols]
            gathered[me, at] = scaled.astype(jnp.bfloat16)
        for j, peer in enumerate(peers):
            send(me, g, peer, far_send.at[j, g]).start()
        send(me, g, sibling, near_send.at[g]).start()

    part, _, links = chaos_values.shape
    total_rows = modes * rows
    per_row = links * part // total_rows
    column_of = lax.broadcasted_iota(jnp.int32, (1, total_rows), 1) // part
    for n in range(links):
        hits[n:n + 1, :] = (column_of == chaos_index[1, n]).astype(jnp.float32)
    lane_of = lax.broadcasted_iota(jnp.int32, (part, total_rows), 1)
    step_of = lax.broadcasted_iota(jnp.int32, (part, total_rows), 0)
    repeat = (lax.rem(lane_of, part) == step_of).astype(jnp.float32).astype(jnp.bfloat16)
    row_of = lax.broadcasted_iota(jnp.int32, (rows, links), 0)
    owner_of = lax.broadcasted_iota(jnp.int32, (rows, links), 1) // per_row
    owned = owner_of == row_of // part + me * (rows // part)
    built = jnp.zeros((rows, total_rows), jnp.float32)
    for i in range(part):
        spread_out = lax.dot_general(
            chaos_values[i], repeat, (((0,), (0,)), ((), ())), preferred_element_type=jnp.float32)
        placed = (spread_out * hits[0:links, :]).astype(jnp.bfloat16)
        mine = jnp.logical_and(owned, lax.rem(row_of, part) == i).astype(jnp.float32).astype(jnp.bfloat16)
        built = built + jnp.dot(mine, placed, preferred_element_type=jnp.float32)
    matrix[...] = built.astype(jnp.bfloat16)

    weight_copy(0).wait()

    @pl.loop(0, groups)
    def _(t):
        g = turn(t)
        right_copy(g).wait()
        sums = stencil(g, 0)
        for b in range(group):
            at = g * group + b
            cols = pl.ds(pl.multiple_of(at * size, size), size)
            rbuf[:, cols] = rbuf[:, cols] - sums[b * rows:(b + 1) * rows] * coef[0:1, cols]

    def mix(g):
        send(sibling, g, sibling, near_send.at[g]).wait_recv()
        for j, peer in enumerate(peers):
            other = peer + 1 - 2 * lax.rem(peer, 2)
            send(other, g, sibling, forward_send.at[j, g]).wait_recv()
        for b in range(group):
            at = g * group + b
            cols = pl.ds(pl.multiple_of(at * size, size), size)
            mixed = jnp.dot(
                matrix[...], gathered[:, at].reshape(modes * rows, size), preferred_element_type=jnp.float32)
            rbuf[:, cols] = rbuf[:, cols] - mixed

    def forward(g):
        for j, peer in enumerate(peers):
            send(peer, g, peer, far_send.at[j, g]).wait_recv()
            send(peer, g, sibling, forward_send.at[j, g]).start()

    forward(turn(0))

    @pl.loop(1, groups)
    def _(t):
        forward(turn(t))
        mix(turn(t - 1))

    mix(turn(groups - 1))

    @pl.loop(0, groups)
    def _(g):
        send(me, g, sibling, near_send.at[g]).wait_send()
        for j, peer in enumerate(peers):
            send(me, g, peer, far_send.at[j, g]).wait_send()
            send(peer, g, sibling, forward_send.at[j, g]).wait_send()

    @pl.when(has_left)
    def _():
        to_left.wait_send()

    @pl.when(has_right)
    def _():
        to_right.wait_send()


def packed_kernel(
    modes, slabs, group, packed,
    field, right, coefficient, blocks, couplings, chaos_values, chaos_index,
    fbuf, rbuf,
    low, weights, coef, gathered, outgoing, arrived, matrix, hits, picks,
    field_sem, right_sem, weight_sem, coef_sem,
    halo_send, halo_recv, near_send, near_recv, far_send, far_recv, forward_send, forward_recv,
):
    rows, width = field.shape
    size = blocks.shape[-1]
    count = width // size
    groups = count // group
    span = group * size
    taps = 2 * REACH + 1
    pairs = modes // 2
    me = lax.axis_index("mode")
    slab = lax.axis_index("mesh")
    sibling = me + 1 - 2 * lax.rem(me, 2)
    peer = lax.rem(me + 2, modes)
    peers = [peer]
    core = lax.rem(me, 2)
    here = me // 2
    there = peer // 2
    share = group // 2
    has_left = slab > 0
    has_right = slab < slabs - 1

    def columns(g):
        return pl.ds(pl.multiple_of(g * span, span), span)

    def field_copy(g):
        return pltpu.make_async_copy(field.at[:, columns(g)], fbuf.at[:, columns(g)], field_sem.at[g])

    def right_copy(g):
        return pltpu.make_async_copy(right.at[:, columns(g)], rbuf.at[:, columns(g)], right_sem.at[g])

    def weight_copy(k):
        return pltpu.make_async_copy(blocks.at[k], weights.at[k], weight_sem.at[k])

    field_copy(0).start()
    field_copy(groups - 1).start()
    weight_copy(1).start()
    coef_copy = pltpu.make_async_copy(coefficient, coef, coef_sem)
    coef_copy.start()

    @pl.loop(1, groups - 1)
    def _(g):
        field_copy(g).start()

    weight_copy(0).start()

    @pl.loop(0, groups)
    def _(g):
        right_copy(g).start()

    barrier = pltpu.get_barrier_semaphore()
    for other in [sibling] + peers:
        pl.semaphore_signal(barrier, inc=1, device_id={"mode": other}, device_id_type=MESH)

    @pl.when(has_left)
    def _():
        pl.semaphore_signal(barrier, inc=1, device_id={"mesh": slab - 1}, device_id_type=MESH)

    @pl.when(has_right)
    def _():
        pl.semaphore_signal(barrier, inc=1, device_id={"mesh": slab + 1}, device_id_type=MESH)

    def lower(g):
        for b in range(group):
            at = g * group + b
            cols = pl.ds(pl.multiple_of(at * size, size), size)
            low[REACH + at] = fbuf[:, cols].astype(jnp.bfloat16)

    part, _, links = chaos_values.shape
    total_rows = modes * rows
    per_row = links * part // total_rows
    column_of = lax.broadcasted_iota(jnp.int32, (1, total_rows), 1) // part
    for n in range(links):
        hits[n:n + 1, :] = (column_of == chaos_index[1, n]).astype(jnp.float32)
    both = 2 * rows
    tall = packed * part
    lanes = lax.broadcasted_iota(jnp.int32, (1, total_rows), 1)
    pair_of_entry = lax.broadcasted_iota(jnp.int32, (links, total_rows), 0) // per_row * part // both
    earlier = jnp.logical_and(
        lax.broadcasted_iota(jnp.int32, (total_rows, total_rows), 0) // part
        < lax.broadcasted_iota(jnp.int32, (total_rows, total_rows), 1) // part,
        jnp.logical_and(
            lax.broadcasted_iota(jnp.int32, (total_rows, total_rows), 0) // both
            == lax.broadcasted_iota(jnp.int32, (total_rows, total_rows), 1) // both,
            lax.rem(lax.broadcasted_iota(jnp.int32, (total_rows, total_rows), 0), part) == 0))
    earlier = earlier.astype(jnp.float32).astype(jnp.bfloat16)

    def picked(source, target):
        wanted = jnp.max(jnp.where(pair_of_entry == target, hits[0:links, :], 0.0), axis=0, keepdims=True)
        wanted = jnp.where(lanes // both == source, wanted, 0.0)
        before = jnp.dot(
            jnp.broadcast_to(wanted, (8, total_rows)).astype(jnp.bfloat16), earlier,
            preferred_element_type=jnp.float32)[0:1]
        place = before * part + lax.rem(lanes, part).astype(jnp.float32)
        row = lax.broadcasted_iota(jnp.int32, (tall, total_rows), 0).astype(jnp.float32)
        return jnp.where(jnp.logical_and(row == place, wanted > 0.0), 1.0, 0.0).astype(jnp.bfloat16)

    picks[...] = picked(here, there)

    field_copy(0).wait()
    lower(0)
    field_copy(groups - 1).wait()
    lower(groups - 1)

    pl.semaphore_wait(barrier, pairs + jnp.minimum(slab, 1) + jnp.minimum(slabs - 1 - slab, 1))

    to_left = pltpu.make_async_remote_copy(
        src_ref=low.at[pl.ds(REACH, REACH)], dst_ref=low.at[pl.ds(REACH + count, REACH)],
        send_sem=halo_send.at[0], recv_sem=halo_recv.at[0],
        device_id={"mesh": slab - 1}, device_id_type=MESH)
    to_right = pltpu.make_async_remote_copy(
        src_ref=low.at[pl.ds(count, REACH)], dst_ref=low.at[pl.ds(0, REACH)],
        send_sem=halo_send.at[1], recv_sem=halo_recv.at[1],
        device_id={"mesh": slab + 1}, device_id_type=MESH)

    @pl.when(has_left)
    def _():
        to_left.start()

    @pl.when(has_right)
    def _():
        to_right.start()

    @pl.when(jnp.logical_not(has_left))
    def _():
        low[pl.ds(0, REACH)] = jnp.zeros((REACH, rows, size), jnp.bfloat16)

    @pl.when(jnp.logical_not(has_right))
    def _():
        low[pl.ds(REACH + count, REACH)] = jnp.zeros((REACH, rows, size), jnp.bfloat16)

    field_copy(1).wait()
    lower(1)
    weight_copy(1).wait()
    coef_copy.wait()

    def stencil(g, k):
        tall = []
        for b in range(group):
            at = g * group + b
            wide = []
            for c in range(taps):
                keep = jnp.full((rows, size), couplings[c, at].astype(jnp.float32)).astype(jnp.bfloat16)
                wide.append(low[at + c] * keep)
            tall.append(jnp.concatenate(wide, axis=1))
        stacked = jnp.concatenate(tall, axis=0)
        return jnp.dot(stacked, weights[k].reshape(taps * size, size), preferred_element_type=jnp.float32)

    def near(g):
        held = gathered.at[core, pl.ds(g * group, group)]
        return pltpu.make_async_remote_copy(
            src_ref=held, dst_ref=held, send_sem=near_send.at[g], recv_sem=near_recv.at[g],
            device_id={"mode": sibling}, device_id_type=MESH)

    def far(g):
        return pltpu.make_async_remote_copy(
            src_ref=outgoing.at[pl.ds(g * share, share)],
            dst_ref=arrived.at[pl.ds(g * group + core * share, share)],
            send_sem=far_send.at[g], recv_sem=far_recv.at[g],
            device_id={"mode": peer}, device_id_type=MESH)

    def relay(g):
        held = arrived.at[pl.ds(g * group + core * share, share)]
        return pltpu.make_async_remote_copy(
            src_ref=held, dst_ref=held, send_sem=forward_send.at[g], recv_sem=forward_recv.at[g],
            device_id={"mode": sibling}, device_id_type=MESH)

    def pack(g):
        near(g).wait_recv()
        chosen = picks[:, pl.ds(pl.multiple_of(here * both, both), both)]
        for b in range(share):
            at = g * group + core * share + b
            outgoing[g * share + b] = jnp.dot(
                chosen, gathered[:, at].reshape(both, size),
                preferred_element_type=jnp.float32).astype(jnp.bfloat16)
        far(g).start()

    def settle(g):
        right_copy(g).wait()
        sums = stencil(g, 0)
        for b in range(group):
            at = g * group + b
            cols = pl.ds(pl.multiple_of(at * size, size), size)
            rbuf[:, cols] = rbuf[:, cols] - sums[b * rows:(b + 1) * rows] * coef[0:1, cols]

    def turn(t):
        return lax.rem(t + 1, groups)

    @pl.loop(0, groups)
    def _(t):
        g = turn(t)

        @pl.when(t + 2 <= groups - 2)
        def _():
            field_copy(t + 2).wait()
            lower(t + 2)

        @pl.when(jnp.logical_and(t == groups - 2, has_right))
        def _():
            to_left.wait_recv()

        @pl.when(jnp.logical_and(t == groups - 1, has_left))
        def _():
            to_right.wait_recv()

        sums = stencil(g, 1)
        for b in range(group):
            at = g * group + b
            cols = pl.ds(pl.multiple_of(at * size, size), size)
            scaled = sums[b * rows:(b + 1) * rows] * coef[1:2, cols]
            gathered[core, at] = scaled.astype(jnp.bfloat16)
        near(g).start()

        @pl.when(t == 1)
        def _():
            weight_copy(0).wait()

        @pl.when(t > 0)
        def _():
            pack(turn(t - 1))
            settle(turn(t - 1))

    pack(turn(groups - 1))
    settle(turn(groups - 1))

    lane_of = lax.broadcasted_iota(jnp.int32, (part, total_rows), 1)
    step_of = lax.broadcasted_iota(jnp.int32, (part, total_rows), 0)
    repeat = (lax.rem(lane_of, part) == step_of).astype(jnp.float32).astype(jnp.bfloat16)
    row_of = lax.broadcasted_iota(jnp.int32, (rows, links), 0)
    owner_of = lax.broadcasted_iota(jnp.int32, (rows, links), 1) // per_row
    owned = owner_of == row_of // part + me * (rows // part)
    built = jnp.zeros((rows, total_rows), jnp.float32)
    for i in range(part):
        spread_out = lax.dot_general(
            chaos_values[i], repeat, (((0,), (0,)), ((), ())), preferred_element_type=jnp.float32)
        placed = (spread_out * hits[0:links, :]).astype(jnp.bfloat16)
        mine = jnp.logical_and(owned, lax.rem(row_of, part) == i).astype(jnp.float32).astype(jnp.bfloat16)
        built = built + jnp.dot(mine, placed, preferred_element_type=jnp.float32)
    built = built.astype(jnp.bfloat16)
    matrix[:, both:both + tall] = lax.dot_general(
        built, picked(there, here), (((1,), (1,)), ((), ())),
        preferred_element_type=jnp.float32).astype(jnp.bfloat16)
    hits[0:rows, :] = built.astype(jnp.float32)
    matrix[:, 0:both] = hits[0:rows, pl.ds(pl.multiple_of(here * both, both), both)].astype(jnp.bfloat16)

    def mix(g):
        relay(g).wait_recv()
        for b in range(group):
            at = g * group + b
            cols = pl.ds(pl.multiple_of(at * size, size), size)
            stacked = jnp.concatenate([gathered[:, at].reshape(both, size), arrived[at]], axis=0)
            mixed = jnp.dot(matrix[...], stacked, preferred_element_type=jnp.float32)
            rbuf[:, cols] = rbuf[:, cols] - mixed

    def forward(g):
        far(g).wait_recv()
        relay(g).start()

    forward(turn(0))

    @pl.loop(1, groups)
    def _(t):
        forward(turn(t))
        mix(turn(t - 1))

    mix(turn(groups - 1))

    @pl.loop(0, groups)
    def _(g):
        near(g).wait_send()
        far(g).wait_send()
        relay(g).wait_send()

    @pl.when(has_left)
    def _():
        to_left.wait_send()

    @pl.when(has_right)
    def _():
        to_right.wait_send()


def finish_kernel(pieces, field, found, precond, updated, residual, stage, sems):
    rows, width = field.shape
    span = width // pieces

    def columns(i):
        return pl.ds(pl.multiple_of(i * span, span), span)

    def found_copy(i):
        return pltpu.make_async_copy(found.at[:, columns(i)], residual.at[:, columns(i)], sems.at[0, i])

    def stage_copy(i):
        return pltpu.make_async_copy(stage.at[:, columns(i)], updated.at[:, columns(i)], sems.at[1, i])

    @pl.loop(0, pieces)
    def _(i):
        found_copy(i).start()
        cols = columns(i)
        stage[:, cols] = field[:, cols] + precond[:, cols] * found[:, cols]
        stage_copy(i).start()

    @pl.loop(0, pieces)
    def _(i):
        found_copy(i).wait()
        stage_copy(i).wait()


def choose_kernel(held, fewest, chaos_index, choice):
    entries = chaos_index.shape[1]
    seen = jnp.int32(0)
    for n in range(entries):
        column = chaos_index[1, n]
        crosses = column // held != n * 2 * held // entries // held
        seen = seen | jnp.where(crosses, jnp.int32(1) << column, 0)
    counts = [sum((seen >> (side * held + i)) & 1 for i in range(held)) for side in range(2)]
    choice[0, 0] = jnp.maximum(jnp.maximum(counts[0], counts[1]) - fewest, 0)


def shards(modes, slabs, field, right_side, coefficient, precond, blocks, couplings, chaos_values, chaos_index):
    rows, width = field.shape
    size = blocks.shape[-1]
    taps = blocks.shape[1]
    count = width // size
    group = 4
    groups = count // group
    others = max(modes // 2 - 1, 1)
    inside = pl.BlockSpec(memory_space=pltpu.VMEM)
    anywhere = pl.BlockSpec(memory_space=pl.ANY)
    spare = 67043328 - 2 * rows * width * 4 - 96 * 1024
    scalars = pl.BlockSpec(memory_space=pltpu.SMEM)
    dma = pltpu.SemaphoreType.DMA
    part = chaos_values.shape[1]
    both = 2 * rows
    entries = chaos_values.shape[0]
    common = [
        pltpu.VMEM((count + 2 * REACH, rows, size), jnp.bfloat16),
        pltpu.VMEM(blocks.shape, jnp.bfloat16),
        pltpu.VMEM(coefficient.shape, jnp.float32),
    ]
    waits = [dma((groups,)), dma((groups,)), dma((2,)), dma, dma((2,)), dma((2,))]
    hits = pltpu.VMEM((max(entries, rows), modes * rows), jnp.float32)

    def whole(*operands):
        return run(
            functools.partial(kernel, modes, slabs, group), 0,
            common + [
                pltpu.VMEM((modes, count, rows, size), jnp.bfloat16),
                pltpu.VMEM((rows, modes * rows), jnp.bfloat16),
                hits,
            ] + waits + [dma((groups,)), dma((others, groups)), dma((others, groups)), dma((modes, groups))],
            operands)

    def reduced(packed, *operands):
        tall = packed * part
        return run(
            functools.partial(packed_kernel, modes, slabs, group, packed), packed,
            common + [
                pltpu.VMEM((2, count, rows, size), jnp.bfloat16),
                pltpu.VMEM((count // 2, tall, size), jnp.bfloat16),
                pltpu.VMEM((count, tall, size), jnp.bfloat16),
                pltpu.VMEM((rows, both + tall), jnp.bfloat16),
                hits,
                pltpu.VMEM((tall, modes * rows), jnp.bfloat16),
            ] + waits + [dma((groups,))] * 6,
            operands)

    def run(body, ident, scratch, operands):
        kept, found = pl.pallas_call(
            body,
            out_shape=[pltpu.VMEM((rows, width), jnp.float32)] * 2,
            in_specs=[anywhere, anywhere, anywhere, anywhere, scalars, inside, scalars],
            out_specs=[inside] * 2,
            scratch_shapes=scratch,
            compiler_params=pltpu.CompilerParams(
                collective_id=ident, has_side_effects=True, vmem_limit_bytes=spare),
            name="gather_mix",
        )(*operands[1:])
        pieces = 16
        return tuple(pl.pallas_call(
            functools.partial(finish_kernel, pieces),
            out_shape=[jax.ShapeDtypeStruct((rows, width), jnp.float32)] * 2,
            in_specs=[inside] * 3,
            out_specs=[anywhere] * 2,
            scratch_shapes=[pltpu.VMEM((rows, width), jnp.float32), dma((2, pieces))],
            compiler_params=pltpu.CompilerParams(vmem_limit_bytes=8 * 1024 * 1024),
            name="finish",
        )(kept, found, operands[0]))

    operands = (
        precond[None, :], field, right_side, coefficient, blocks, couplings.T,
        chaos_values.transpose(1, 2, 0), chaos_index.T)
    if modes != 4 or both % part:
        return whole(*operands)
    held = both // part
    fewest = held // 2 + 1
    choice = pl.pallas_call(
        functools.partial(choose_kernel, held, fewest),
        out_shape=jax.ShapeDtypeStruct((1, 1), jnp.int32),
        in_specs=[scalars],
        out_specs=scalars,
        name="choose",
    )(operands[-1])
    return lax.switch(
        choice[0, 0],
        [functools.partial(reduced, packed) for packed in range(fewest, held + 1)],
        *operands)


def solution(mesh):
    placed = (
        P("mode", "mesh"),
        P("mode", "mesh"),
        P(None, "mesh"),
        P("mesh"),
        P(),
        P("mesh", None),
        P(),
        P(),
    )
    return jax.shard_map(
        functools.partial(shards, mesh.shape["mode"], mesh.shape["mesh"]),
        mesh=mesh,
        in_specs=placed,
        out_specs=(P("mode", "mesh"), P("mode", "mesh")),
        check_vma=False,
    )
```
